32 devices in a mesh: samples: 16 (over z, y, core), feat: 2 (over x).
Axes of the slice: x: 2, y: 2, z: 4, core: 2. Of those that a mesh axis runs over, the one named last changes fastest.
Arguments:
- samples: float32 [4096, 4096], P('samples', 'feat'), may hold values from -12 to 12, as said below
- factor: float32 [4096, 512], P('feat'), may hold values from -6 to 6
Outputs:
- new_factor: float32 [4096, 512], P('feat')
The draws below stay inside these ranges and needn't reach their ends.
Inputs may be any that keep to these rules, and one draw needn't show every extreme that they name: `samples`: Real-valued data.
All inputs are finite; a program needn't handle non-finite values.
Results may differ from the reference program's by a relative error of at most 0.00007.
Values sent between devices are 32-bit elements; how exact they have to be, the bound alone decides.
No kernel may reach another device: no remote copies, remote signals or barrier semaphores. Data moves between devices by JAX's collectives and lax.ppermute only.
A program may use at most 64 MiB of HBM per device.

```python
import jax
import jax.numpy as jnp
from jax import lax

D = 4096
R = 512
NROWS = 4096


def draw_samples(key, part):
    key_scale, key_main, key_skew, key_coef = jax.random.split(jax.random.fold_in(key, 11), 4)
    position = jnp.arange(D, dtype=jnp.float32) / D
    spread = jax.random.uniform(key_scale, (D,), jnp.float32)
    scales = 10.0 ** (0.5 * position + 0.5 * spread - 0.5)
    coefs = jax.random.uniform(key_coef, (D,), jnp.float32, 0.2, 0.6)
    skewed = jnp.clip(jax.random.normal(key_skew, (NROWS, D), jnp.float32), -4.0, 4.0)
    main = jnp.clip(jax.random.normal(key_main, (NROWS, D), jnp.float32), -5.0, 5.0)
    values = scales[None, :] * (main + coefs[None, :] * (skewed * skewed - 1.0))
    return jnp.clip(values, -12.0, 12.0)


def level_of(rng, shape, shards, smallest, largest):
    factor_of = 1.0
    for dim, shards_of in shards:
        steps = jax.random.uniform(jax.random.fold_in(jax.random.fold_in(rng, 6), dim), (shards_of,), jnp.float32, smallest / len(shards), largest / len(shards))
        factor_of = factor_of * jnp.repeat(jnp.exp(steps), shape[dim] // shards_of).reshape((-1,) + (1,) * (len(shape) - 1 - dim))
    return factor_of


def scatter_about(rng, extent, scale, reach, cuts=(), kind=jnp.bfloat16):
    entries = scale * jax.random.normal(rng, extent, jnp.float32)
    if cuts:
        entries = entries * level_of(rng, extent, cuts, -0.22, 0.18)
    return jnp.clip(entries, -reach, reach).astype(kind)


def setup_inputs(seed: int = 0) -> dict:
    arg_keys = jax.random.split(jax.random.key(seed), 3)
    return {
        "samples": draw_samples(jax.random.fold_in(arg_keys[2], 71), 0),
        "factor": scatter_about(arg_keys[1], (D, R), 1.0, 6.0, ((0, 2),), jnp.float32),
    }


def reference(samples, factor):
    high = lax.Precision.HIGHEST
    scaled = factor * (1.0 / jnp.sqrt(jnp.float32(D)))
    proj = jnp.dot(samples, scaled, precision=high, preferred_element_type=jnp.float32)
    squared = proj * proj
    moment = lax.dot_general(samples, squared, (((0,), (0,)), ((), ())), precision=high, preferred_element_type=jnp.float32) / NROWS
    gram = lax.dot_general(scaled, scaled, (((0,), (0,)), ((), ())), precision=high, preferred_element_type=jnp.float32)
    gram_term = jnp.dot(scaled, gram * gram, precision=high, preferred_element_type=jnp.float32)
    grad = 6.0 / jnp.sqrt(jnp.float32(D)) * (gram_term - moment)
    rms = jnp.sqrt(jnp.sum(grad * grad) / (D * R)) + 1e-06
    return factor - 0.5 * grad / rms
```

```python
import functools

import jax
import jax.numpy as jnp
from jax import lax
from jax.experimental import pallas as pl
from jax.experimental.pallas import tpu as pltpu
from jax.sharding import PartitionSpec as P

HIGH = lax.Precision.HIGH
LANES = 128


def dot(a, b, contract):
    return lax.dot_general(
        a, b, (contract, ((), ())), precision=HIGH, preferred_element_type=jnp.float32
    )


def update_kernel(places, step_ref, factor_ref, *refs):
    blocks, out_ref = refs[:-1], refs[-1]
    step = step_ref[0]
    for n, block in enumerate(blocks):
        rows, cols = block.shape
        here = (
            pl.ds(pl.multiple_of(places[2 * n], rows), rows),
            pl.ds(pl.multiple_of(places[2 * n + 1], cols), cols),
        )
        out_ref[here] = factor_ref[here] - step * block[...]


def per_device(samples, factor):
    features, rank = factor.shape
    n = lax.axis_size("samples")
    halves = lax.axis_size("feat")
    depth = n // 4
    rows = features // depth
    cols = rank // 4
    me = lax.axis_index("samples")
    core, y, z = me % 2, (me // 2) % 2, me // 4

    def swap(x, bit):
        return lax.ppermute(x, "samples", [(i, i ^ bit) for i in range(n)])

    def sum_feat(x):
        total = x
        for shift in range(1, halves):
            total = total + lax.ppermute(
                x, "feat", [(i, (i + shift) % halves) for i in range(halves)]
            )
        return total

    def columns(x, block):
        return lax.dynamic_slice_in_dim(x, block * cols, cols, 1)

    root = jnp.sqrt(jnp.float32(features * halves))
    scaled = factor * (1.0 / root)
    mine, theirs = 2 * core + y, 2 * core + 1 - y

    other = swap(samples, 1)
    scaled_mine, scaled_theirs = columns(scaled, mine), columns(scaled, theirs)
    squared = {}
    for name, part in (("theirs", scaled_theirs), ("mine", scaled_mine)):
        proj = sum_feat(
            jnp.concatenate([dot(samples, part, ((1,), (0,))), dot(other, part, ((1,), (0,)))])
        )
        squared[name] = proj * proj

    gram = sum_feat(dot(scaled, scaled_mine, ((0,), (0,))))

    kept = {}
    for k in range(depth - 1, -1, -1):
        at = (z ^ k) * rows
        own = lax.dynamic_slice_in_dim(samples, at, rows, 1)
        oth = lax.dynamic_slice_in_dim(other, at, rows, 1)
        half = own.shape[0]

        def moment_of(sq):
            return dot(own, sq[:half], ((0,), (0,))) + dot(oth, sq[half:], ((0,), (0,)))

        arrived = swap(moment_of(squared["theirs"]), 2)
        kept[k] = arrived + moment_of(squared["mine"])
    total = kept[0]
    for k in range(depth - 1, 0, -1):
        total = total + swap(kept[k], 4 * k)

    moment = total / (samples.shape[0] * n)
    gram_term = dot(
        lax.dynamic_slice_in_dim(scaled, z * rows, rows, 0), gram * gram, ((1,), (0,))
    )
    grad = (6.0 / root) * (gram_term - moment)
    sum_sq = lax.psum(jnp.sum(grad * grad), ("samples", "feat"))
    rms = jnp.sqrt(sum_sq / (features * halves * rank)) + 1e-06
    step = (0.5 / rms).reshape(1)

    blocks, places = [], []
    for k in range(depth):
        here = grad if k == 0 else swap(grad, 4 * k)
        for j in range(2):
            block = here if j == 0 else swap(here, 2)
            for i in range(2):
                blocks.append(block if i == 0 else swap(block, 1))
                places += [(z ^ k) * rows, (2 * (core ^ i) + (y ^ j)) * cols]
    vmem = pl.BlockSpec(memory_space=pltpu.VMEM)
    smem = pl.BlockSpec(memory_space=pltpu.SMEM)
    return pl.pallas_call(
        update_kernel,
        out_shape=jax.ShapeDtypeStruct(factor.shape, factor.dtype),
        in_specs=[smem, smem, vmem] + [vmem] * len(blocks),
        out_specs=vmem,
        name="update",
    )(jnp.stack(places), step, factor, *blocks)


def solution(mesh):
    placed = (P("samples", "feat"), P("feat", None))
    return jax.shard_map(
        per_device, mesh=mesh, in_specs=placed, out_specs=P("feat", None), check_vma=False
    )
```

```python
import functools

import jax
import jax.numpy as jnp
from jax import lax
from jax.experimental import pallas as pl
from jax.experimental.pallas import tpu as pltpu
from jax.sharding import PartitionSpec as P


TILE = (8, 128)
CHUNKS = 4
WIDE, NARROW = jnp.float32, jnp.bfloat16


def after(x, *first):
    return lax.optimization_barrier((x,) + first)[0]


def position():
    me = lax.axis_index("samples")
    return me & 1, (me >> 1) & 1, me >> 2


def block(index, size):
    return pl.ds(pl.multiple_of(index * size, size), size)


def split(x):
    high = x.astype(NARROW)
    return high, (x - high.astype(WIDE)).astype(NARROW)


def matmul(a, b, contract=((1,), (0,))):
    return lax.dot_general(a, b, (contract, ((), ())), preferred_element_type=WIDE)


def three_pass(a_high, a_low, pair):
    cols = pair.shape[1] // 2
    wide = matmul(a_high, pair)
    return wide[:, :cols] + (wide[:, cols:] + matmul(a_low, pair[:, :cols]))


def fetch(source, held, sem):
    copy = pltpu.make_async_copy(source, held, sem)
    copy.start()
    return copy


def own_kernel(kept, samples_ref, factor_ref, proj_ref, pair_ref, *refs):
    *more, held_x, held_f, sem = refs
    core, y, _ = position()
    cols = held_f.shape[1]
    here = block(2 * core + (y if kept else 1 - y), cols)
    step = held_x.shape[1] // CHUNKS
    copies = []
    for n in range(CHUNKS):
        part = pl.ds(n * step, step)
        copies.append(fetch(factor_ref.at[part, here], held_f.at[part], sem.at[0, n]))
        copies.append(fetch(samples_ref.at[:, part], held_x.at[:, part], sem.at[1, n]))
    total = None
    for n in range(CHUNKS):
        part = pl.ds(n * step, step)
        copies[2 * n].wait()
        f = held_f[part]
        pair = jnp.concatenate(split(f), axis=1)
        pair_ref[part] = pair
        copies[2 * n + 1].wait()
        x = held_x[:, part]
        add = three_pass(*split(x), pair)
        total = add if total is None else total + add
        if kept:
            high_ref, low_ref, turned_ref = more
            high_ref[part], low_ref[part] = split(x.T)
            turned_ref[:cols, part], turned_ref[cols:, part] = split(f.T)
    proj_ref[...] = total


def other_kernel(samples_ref, pair_ref, proj_ref, held_x, sem):
    step = held_x.shape[1] // CHUNKS
    parts = [pl.ds(n * step, step) for n in range(CHUNKS)]
    copies = [
        fetch(samples_ref.at[:, part], held_x.at[:, part], sem.at[n])
        for n, part in enumerate(parts)
    ]
    total = None
    for part, copy in zip(parts, copies):
        copy.wait()
        add = three_pass(*split(held_x[:, part]), pair_ref[part])
        total = add if total is None else total + add
    proj_ref[...] = total


def both_kernel(samples_ref, pair_ref, own_ref, both_ref, high_ref, low_ref, held_x, sem):
    step = held_x.shape[1] // CHUNKS
    parts = [pl.ds(n * step, step) for n in range(CHUNKS)]
    copies = [
        fetch(samples_ref.at[:, part], held_x.at[:, part], sem.at[n])
        for n, part in enumerate(parts)
    ]
    count = own_ref.shape[0]
    both_ref[:count] = own_ref[...]
    total = None
    for part, copy in zip(parts, copies):
        copy.wait()
        x = held_x[:, part]
        add = three_pass(*split(x), pair_ref[part])
        total = add if total is None else total + add
        high_ref[part], low_ref[part] = split(x.T)
    both_ref[count:] = total


def moment_kernel(scale, starts, k, *refs):
    *projs, own_h, own_l, oth_h, oth_l, out_ref = refs
    rows, count = out_ref.shape[0], own_h.shape[1]
    here = block(position()[2] ^ k, rows)
    total = None
    for n, (h, l) in enumerate(((own_h, own_l), (oth_h, oth_l))):
        a, b = projs[2 * n : 2 * n + 2] if len(projs) == 4 else projs
        start = starts[n]
        proj = (a[start : start + count] + b[start : start + count]) * scale
        pair = jnp.concatenate(split(proj * proj), axis=1)
        part = three_pass(h[here, :], l[here, :], pair)
        total = part if total is None else total + part
    out_ref[...] = total


def gram_kernel(factor_ref, turned_ref, out_ref, held, sem):
    step = held.shape[0] // CHUNKS
    parts = [pl.ds(n * step, step) for n in range(CHUNKS)]
    copies = [
        fetch(factor_ref.at[part], held.at[part], sem.at[n]) for n, part in enumerate(parts)
    ]
    cols = out_ref.shape[0]
    total = None
    for part, copy in zip(parts, copies):
        copy.wait()
        high, low = split(held[part])
        tall = matmul(turned_ref[:, part], high)
        add = tall[:cols] + (tall[cols:] + matmul(turned_ref[:cols, part], low))
        total = add if total is None else total + add
    out_ref[...] = total


def term_kernel(scale, factor_ref, a_ref, b_ref, out_ref, held, sem):
    fetch(factor_ref.at[block(position()[2], held.shape[0])], held, sem).wait()
    gram = (a_ref[...] + b_ref[...]) * (scale * scale)
    cols = gram.shape[0]
    tall = jnp.concatenate(split(gram * gram), axis=0)
    high, low = split(held[...])
    nt = ((1,), (1,))
    wide = matmul(high, tall, nt)
    out_ref[...] = (
        wide[:, :cols] + (wide[:, cols:] + matmul(low, tall[:cols], nt))
    ) * scale


def grad_kernel(coef, total_rows, term_ref, *refs):
    *parts, grad_ref, sums_ref = refs
    total = parts[0][...]
    for part in parts[1:]:
        total = total + part[...]
    grad = coef * (term_ref[...] - total / total_rows)
    grad_ref[...] = grad
    down = jnp.sum(grad * grad, axis=0, keepdims=True)
    sums_ref[...] = jnp.broadcast_to(jnp.sum(down, axis=1, keepdims=True), sums_ref.shape)


def update_kernel(places, fresh, entries, rows, cols, sums_a, sums_b, factor_ref, *refs):
    count = len(places)
    blocks = refs[:count]
    out_ref, held, got, in_sem, block_sem, out_sem = refs[count + (not fresh) :]
    core, y, z = position()
    slabs = count // 4

    def slab(s):
        return block(z ^ places[4 * s][0], rows)

    loads, fetches = [], []
    for s in range(slabs):
        loads.append(fetch(factor_ref.at[slab(s)], held.at[s], in_sem.at[s]))
        for b in range(4 * s, 4 * s + 4):
            fetches.append(fetch(blocks[b], got.at[b], block_sem.at[b]))
    rms = jnp.sqrt((sums_a[...] + sums_b[...]) / entries) + 1e-06
    step = (0.5 / rms)[0:1, 0:1]
    stores = []
    for s in range(slabs):
        loads[s].wait()
        for b in range(4 * s, 4 * s + 4):
            fetches[b].wait()
            _, j, i = places[b]
            here = block(2 * (core ^ i) + (y ^ j), cols)
            held[s, :, here] = held[s, :, here] - step * got[b]
        stores.append(fetch(held.at[s], out_ref.at[slab(s)], out_sem.at[s]))
    for store in stores:
        store.wait()


def in_hbm(x):
    return pltpu.with_memory_space_constraint(x, pltpu.HBM)


VMEM, HBM = pl.BlockSpec(memory_space=pltpu.VMEM), pl.BlockSpec(memory_space=pltpu.HBM)


def update(places, sums, factor, blocks, entries, rows, cols, out=None):
    count = len(blocks)
    slabs = count // 4
    fresh = out is None
    return pl.pallas_call(
        functools.partial(update_kernel, places, fresh, entries, rows, cols),
        out_shape=jax.ShapeDtypeStruct(factor.shape, factor.dtype),
        in_specs=[VMEM, VMEM, HBM]
        + [pl.BlockSpec(memory_space=pl.ANY)] * count
        + [HBM] * (not fresh),
        out_specs=HBM,
        input_output_aliases={} if fresh else {3 + count: 0},
        scratch_shapes=[
            pltpu.VMEM((slabs, rows, factor.shape[1]), WIDE),
            pltpu.VMEM((count, rows, cols), WIDE),
            pltpu.SemaphoreType.DMA((slabs,)),
            pltpu.SemaphoreType.DMA((count,)),
            pltpu.SemaphoreType.DMA((slabs,)),
        ],
        compiler_params=pltpu.CompilerParams(vmem_limit_bytes=12 << 20),
        name="update",
    )(*sums, in_hbm(factor), *blocks, *([] if fresh else [out]))


def call(kernel, inputs, outputs, grant, hbm=(), scratch=()):
    return pl.pallas_call(
        kernel,
        out_shape=[jax.ShapeDtypeStruct(shape, kind) for shape, kind in outputs],
        in_specs=[HBM if i in hbm else VMEM for i in range(len(inputs))],
        out_specs=[VMEM] * len(outputs),
        scratch_shapes=list(scratch),
        compiler_params=pltpu.CompilerParams(vmem_limit_bytes=grant << 20),
    )(*[in_hbm(x) if i in hbm else x for i, x in enumerate(inputs)])


def low_bit(k):
    return k & -k


def step_of(samples, factor):
    features, rank = factor.shape
    count = samples.shape[0]
    n = lax.axis_size("samples")
    halves = lax.axis_size("feat")
    full = features * halves
    depth = n // 4
    rows = features // depth
    cols = rank // 4

    def swap(x, bit):
        return lax.ppermute(x, "samples", [(i, i ^ bit) for i in range(n)])

    def across(x):
        return lax.ppermute(x, "feat", [(i, (i + 1) % halves) for i in range(halves)])

    proj_of, pair_of = ((count, cols), WIDE), ((features, 2 * cols), NARROW)
    turned = ((features, count), NARROW)
    flipped = ((2 * cols, features), NARROW)
    block_of = ((rows, cols), WIDE)
    held_x = [pltpu.VMEM(samples.shape, WIDE)]
    held_f = [pltpu.VMEM((features, cols), WIDE)]
    dmas = [pltpu.SemaphoreType.DMA((CHUNKS,))]
    two_dmas = [pltpu.SemaphoreType.DMA((2, CHUNKS))]

    other = swap(samples, 1)
    own_t, pair_t = call(
        functools.partial(own_kernel, False), [samples, factor],
        [proj_of, pair_of], 12, (0, 1), held_x + held_f + two_dmas,
    )
    own_t2 = across(own_t)
    (oth_t,) = call(other_kernel, [other, pair_t], [proj_of], 10, (0,), held_x + dmas)
    oth_t2 = across(oth_t)
    own_m, pair_m, own_h, own_l, turned_m = call(
        functools.partial(own_kernel, True), [after(samples, oth_t), factor],
        [proj_of, pair_of, turned, turned, flipped], 14, (0, 1), held_x + held_f + two_dmas,
    )
    both, oth_h, oth_l = call(
        both_kernel, [other, pair_m, own_m],
        [((2 * count, cols), WIDE), turned, turned], 12, (0,), held_x + dmas,
    )
    both2 = across(both)

    def moment_of(k, projs, starts):
        return call(
            functools.partial(moment_kernel, full**-0.5, starts, k),
            [*projs, own_h, own_l, oth_h, oth_l], [block_of], 8,
        )[0]

    order = range(depth - 1, -1, -1)
    arrived, kept = {}, {}
    last = both
    for k in order:
        last = moment_of(k, [after(own_t, last), own_t2, oth_t, oth_t2], (0, 0))
        arrived[k] = swap(last, 2)
    for k in order:
        kept[k] = last = moment_of(k, [after(both, last), both2], (0, count))
    (gram,) = call(
        gram_kernel, [factor, after(turned_m, last)], [((cols, rank), WIDE)], 10, (0,),
        [pltpu.VMEM(factor.shape, WIDE)] + dmas,
    )
    (term,) = call(
        functools.partial(term_kernel, full**-0.5),
        [factor, gram, across(gram)], [block_of], 8, (0,),
        [pltpu.VMEM((rows, rank), WIDE), pltpu.SemaphoreType.DMA],
    )
    parts = {k: [kept[k], arrived[k]] for k in order}
    for k in order:
        if k:
            if k + 1 < depth:
                parts[k][1] = after(arrived[k], previous)
            previous = parts[k][0]
            for part in parts[k][1:]:
                previous = previous + part
            bit = low_bit(k)
            parts[k ^ bit].append(swap(previous, 4 * bit))
    grad, sums = call(
        functools.partial(grad_kernel, 6.0 / full**0.5, count * n),
        [term, *parts[0]], [block_of, (TILE, WIDE)], 8,
    )
    sums = sums + across(sums)
    bit = depth // 2
    while bit:
        sums = sums + swap(sums, 4 * bit)
        bit //= 2
    sums = sums + swap(sums, 2)
    sums = (sums, swap(sums, 1))

    held = {0: grad}
    bit = depth // 2
    while bit:
        for k in sorted(held):
            held[k ^ bit] = swap(held[k], 4 * bit)
        bit //= 2
    out = None
    for group in (range(depth - 1), (depth - 1,)):
        blocks, places = [], []
        for k in group:
            for j, value in enumerate((held[k], swap(held[k], 2))):
                blocks += [value, swap(value, 1)]
                places += [(k, j, 0), (k, j, 1)]
        out = update(places, sums, factor, blocks, full * rank, rows, cols, out)
    return out


def solution(mesh):
    placed = (P("samples", "feat"), P("feat", None))
    return jax.shard_map(
        step_of, mesh=mesh, in_specs=placed, out_specs=P("feat", None), check_vma=False
    )
```

```python
import functools

import jax
import jax.numpy as jnp
from jax import lax
from jax.experimental import pallas as pl
from jax.experimental.pallas import tpu as pltpu
from jax.sharding import PartitionSpec as P


TILE = (8, 128)
CHUNKS = 4
WIDE, NARROW = jnp.float32, jnp.bfloat16


def after(x, *first):
    return lax.optimization_barrier((x,) + first)[0]


def position():
    me = lax.axis_index("samples")
    return me & 1, (me >> 1) & 1, me >> 2


def block(index, size):
    return pl.ds(pl.multiple_of(index * size, size), size)


def split(x):
    high = x.astype(NARROW)
    return high, (x - high.astype(WIDE)).astype(NARROW)


def matmul(a, b, contract=((1,), (0,))):
    return lax.dot_general(a, b, (contract, ((), ())), preferred_element_type=WIDE)


def three_pass(a_high, a_low, pair):
    cols = pair.shape[1] // 2
    wide = matmul(a_high, pair)
    return wide[:, :cols] + (wide[:, cols:] + matmul(a_low, pair[:, :cols]))


def fetch(source, held, sem):
    copy = pltpu.make_async_copy(source, held, sem)
    copy.start()
    return copy


def own_kernel(kept, samples_ref, factor_ref, *refs):
    proj_ref, pair_ref, *turned, held_x, held_f, sem = refs[kept:]
    core, y, _ = position()
    cols = proj_ref.shape[1]
    here = block(2 * core + (y if kept else 1 - y), cols)
    step = held_x.shape[1] // CHUNKS
    parts = [pl.ds(n * step, step) for n in range(CHUNKS)]
    copies = []
    for n, part in enumerate(parts):
        copies.append(fetch(factor_ref.at[part, here], held_f.at[part], sem.at[0, n]))
        copies.append(fetch(samples_ref.at[:, part], held_x.at[:, part], sem.at[1, n]))
    total = None
    for n, part in enumerate(parts):
        copies[2 * n].wait()
        pair = jnp.concatenate(split(held_f[part]), axis=1)
        pair_ref[part] = pair
        copies[2 * n + 1].wait()
        x = held_x[:, part]
        add = three_pass(*split(x), pair)
        total = add if total is None else total + add
        if kept:
            turned[0][part], turned[1][part] = split(x.T)
    proj_ref[...] = total


def other_kernel(samples_ref, pair_ref, proj_ref):
    proj_ref[...] = three_pass(*split(samples_ref[...]), pair_ref[...])


def both_kernel(samples_ref, pair_ref, own_ref, both_ref, high_ref, low_ref):
    count = own_ref.shape[0]
    x = samples_ref[...]
    both_ref[:count] = own_ref[...]
    both_ref[count:] = three_pass(*split(x), pair_ref[...])
    high_ref[...], low_ref[...] = split(x.T)


def moment_kernel(scale, starts, k, *refs):
    *projs, own_h, own_l, oth_h, oth_l, out_ref = refs
    rows, count = out_ref.shape[0], own_h.shape[1]
    here = block(position()[2] ^ k, rows)
    total = None
    for n, (h, l) in enumerate(((own_h, own_l), (oth_h, oth_l))):
        a, b = projs[2 * n : 2 * n + 2] if len(projs) == 4 else projs
        start = starts[n]
        proj = (a[start : start + count] + b[start : start + count]) * scale
        pair = jnp.concatenate(split(proj * proj), axis=1)
        part = three_pass(h[here, :], l[here, :], pair)
        total = part if total is None else total + part
    out_ref[...] = total


def gram_kernel(factor_ref, _, out_ref, held, sem):
    core, y, _ = position()
    cols = out_ref.shape[0]
    here = block(2 * core + y, cols)
    step = held.shape[0] // CHUNKS
    parts = [pl.ds(n * step, step) for n in range(CHUNKS)]
    copies = [
        fetch(factor_ref.at[part], held.at[part], sem.at[n]) for n, part in enumerate(parts)
    ]
    total = None
    for part, copy in zip(parts, copies):
        copy.wait()
        high, low = split(held[part])
        left = jnp.concatenate(split(held[part, here].T), axis=0)
        tall = matmul(left, high)
        add = tall[:cols] + (tall[cols:] + matmul(left[:cols], low))
        total = add if total is None else total + add
    out_ref[...] = total


def term_kernel(scale, factor_ref, a_ref, b_ref, out_ref, held, sem):
    fetch(factor_ref.at[block(position()[2], held.shape[0])], held, sem).wait()
    gram = (a_ref[...] + b_ref[...]) * (scale * scale)
    cols = gram.shape[0]
    tall = jnp.concatenate(split(gram * gram), axis=0)
    high, low = split(held[...])
    nt = ((1,), (1,))
    wide = matmul(high, tall, nt)
    out_ref[...] = (
        wide[:, :cols] + (wide[:, cols:] + matmul(low, tall[:cols], nt))
    ) * scale


def add_kernel(*refs):
    *parts, out_ref = refs
    total = parts[0][...]
    for part in parts[1:]:
        total = total + part[...]
    out_ref[...] = total


def grad_kernel(coef, total_rows, term_ref, *refs):
    *parts, grad_ref, sums_ref = refs
    total = parts[0][...]
    for part in parts[1:]:
        total = total + part[...]
    grad = coef * (term_ref[...] - total / total_rows)
    grad_ref[...] = grad
    down = jnp.sum(grad * grad, axis=0, keepdims=True)
    sums_ref[...] = jnp.broadcast_to(jnp.sum(down, axis=1, keepdims=True), sums_ref.shape)


def step_of(sums_a, sums_b, entries):
    rms = jnp.sqrt((sums_a[...] + sums_b[...]) / entries) + 1e-06
    return (0.5 / rms)[0:1, 0:1]


def columns_at(place, cols):
    core, y, _ = position()
    return block(2 * (core ^ place[2]) + (y ^ place[1]), cols)


def early_kernel(places, late, entries, rows, cols, sums_a, sums_b, factor_ref, *refs):
    count = len(places)
    blocks = refs[:count]
    out_ref, late_ref, held, got, in_sem, block_sem, out_sem = refs[count:]
    slabs = sorted({place[0] for place in places})

    def slab(k):
        return block(position()[2] ^ k, rows)

    loads = [fetch(factor_ref.at[slab(k)], held.at[s], in_sem.at[s]) for s, k in enumerate(slabs)]
    fetches = [fetch(blocks[b], got.at[b], block_sem.at[b]) for b in range(count)]
    step = step_of(sums_a, sums_b, entries)
    stores = []
    for s, k in enumerate(slabs):
        loads[s].wait()
        for b, place in enumerate(places):
            if place[0] == k:
                fetches[b].wait()
                here = columns_at(place, cols)
                held[s, :, here] = held[s, :, here] - step * got[b]
        for n, place in enumerate(late):
            if place[0] == k:
                late_ref[n] = held[s, :, columns_at(place, cols)]
        stores.append(fetch(held.at[s], out_ref.at[slab(k)], out_sem.at[s]))
    for store in stores:
        store.wait()


def late_kernel(places, entries, sums_a, sums_b, late_ref, *refs):
    count = len(places)
    blocks = refs[:count]
    _, out_ref, done, out_sem = refs[count:]
    step = step_of(sums_a, sums_b, entries)
    stores = []
    for b, place in enumerate(places):
        done[b] = late_ref[b] - step * blocks[b][...]
        rows, cols = blocks[b].shape
        at = (block(position()[2] ^ place[0], rows), columns_at(place, cols))
        stores.append(fetch(done.at[b], out_ref.at[at], out_sem.at[b]))
    for store in stores:
        store.wait()


def in_hbm(x):
    return pltpu.with_memory_space_constraint(x, pltpu.HBM)


VMEM, HBM = pl.BlockSpec(memory_space=pltpu.VMEM), pl.BlockSpec(memory_space=pltpu.HBM)


def early_update(places, late, sums, factor, blocks, entries):
    count, (rows, cols) = len(blocks), blocks[0].shape
    slabs = len({place[0] for place in places})
    return pl.pallas_call(
        functools.partial(early_kernel, places, late, entries, rows, cols),
        out_shape=[
            jax.ShapeDtypeStruct(factor.shape, WIDE),
            jax.ShapeDtypeStruct((len(late), rows, cols), WIDE),
        ],
        in_specs=[VMEM, VMEM, HBM] + [pl.BlockSpec(memory_space=pl.ANY)] * count,
        out_specs=[HBM, VMEM],
        scratch_shapes=[
            pltpu.VMEM((slabs, rows, factor.shape[1]), WIDE),
            pltpu.VMEM((count, rows, cols), WIDE),
            pltpu.SemaphoreType.DMA((slabs,)),
            pltpu.SemaphoreType.DMA((count,)),
            pltpu.SemaphoreType.DMA((slabs,)),
        ],
        compiler_params=pltpu.CompilerParams(vmem_limit_bytes=14 << 20),
        name="early",
    )(*sums, in_hbm(factor), *blocks)


def late_update(places, sums, late, blocks, out, entries):
    count = len(blocks)
    return pl.pallas_call(
        functools.partial(late_kernel, places, entries),
        out_shape=jax.ShapeDtypeStruct(out.shape, WIDE),
        in_specs=[VMEM] * (3 + count) + [HBM],
        out_specs=HBM,
        input_output_aliases={3 + count: 0},
        scratch_shapes=[
            pltpu.VMEM(late.shape, WIDE),
            pltpu.SemaphoreType.DMA((count,)),
        ],
        compiler_params=pltpu.CompilerParams(vmem_limit_bytes=8 << 20),
        name="late",
    )(*sums, late, *blocks, out)


def call(kernel, inputs, outputs, grant, hbm=(), scratch=()):
    return pl.pallas_call(
        kernel,
        out_shape=[jax.ShapeDtypeStruct(shape, kind) for shape, kind in outputs],
        in_specs=[HBM if i in hbm else VMEM for i in range(len(inputs))],
        out_specs=[VMEM] * len(outputs),
        scratch_shapes=list(scratch),
        compiler_params=pltpu.CompilerParams(vmem_limit_bytes=grant << 20),
    )(*[in_hbm(x) if i in hbm else x for i, x in enumerate(inputs)])


def low_bit(k):
    return k & -k


def gradient_step(samples, factor):
    features, rank = factor.shape
    count = samples.shape[0]
    n = lax.axis_size("samples")
    halves = lax.axis_size("feat")
    full = features * halves
    depth = n // 4
    rows = features // depth
    cols = rank // 4

    def swap(x, bit):
        return lax.ppermute(x, "samples", [(i, i ^ bit) for i in range(n)])

    def across(x):
        return lax.ppermute(x, "feat", [(i, (i + 1) % halves) for i in range(halves)])

    proj_of, pair_of = ((count, cols), WIDE), ((features, 2 * cols), NARROW)
    turned = ((features, count), NARROW)
    block_of = ((rows, cols), WIDE)
    held_x = [pltpu.VMEM(samples.shape, WIDE)]
    held_f = [pltpu.VMEM((features, cols), WIDE)]
    dmas = [pltpu.SemaphoreType.DMA((CHUNKS,))]
    two_dmas = [pltpu.SemaphoreType.DMA((2, CHUNKS))]

    other = swap(samples, 1)
    own_t, pair_t = call(
        functools.partial(own_kernel, False), [samples, factor], [proj_of, pair_of],
        12, (0, 1), held_x + held_f + two_dmas,
    )
    own_t2 = across(own_t)
    (oth_t,) = call(other_kernel, [other, pair_t], [proj_of], 8)
    oth_t2 = across(oth_t)
    own_m, pair_m, own_h, own_l = call(
        functools.partial(own_kernel, True), [samples, factor, oth_t],
        [proj_of, pair_of, turned, turned], 12, (0, 1), held_x + held_f + two_dmas,
    )
    both, oth_h, oth_l = call(
        both_kernel, [other, pair_m, own_m],
        [((2 * count, cols), WIDE), turned, turned], 10,
    )
    both2 = across(both)

    def moment_of(k, projs, starts):
        return call(
            functools.partial(moment_kernel, full**-0.5, starts, k),
            [*projs, own_h, own_l, oth_h, oth_l], [block_of], 8,
        )[0]

    order = range(depth - 1, -1, -1)
    arrived, kept = {}, {}
    for k in order:
        last = moment_of(k, [own_t, own_t2, oth_t, oth_t2], (0, 0))
        arrived[k] = swap(last, 2)
    for k in order:
        kept[k] = last = moment_of(k, [after(both, last), both2], (0, count))
    (gram,) = call(
        gram_kernel, [factor, last], [((cols, rank), WIDE)], 10, (0,),
        [pltpu.VMEM(factor.shape, WIDE)] + dmas,
    )
    (term,) = call(
        functools.partial(term_kernel, full**-0.5),
        [factor, gram, across(gram)], [block_of], 8, (0,),
        [pltpu.VMEM((rows, rank), WIDE), pltpu.SemaphoreType.DMA],
    )

    def sum_of(*parts):
        return call(add_kernel, parts, [(parts[0].shape, WIDE)], 4)[0]

    parts = {k: [kept[k], arrived[k]] for k in order}
    for k in order:
        if k:
            bit = low_bit(k)
            parts[k ^ bit].append(swap(sum_of(*parts[k]), 4 * bit))
    grad, sums = call(
        functools.partial(grad_kernel, 6.0 / full**0.5, count * n),
        [term, *parts[0]], [block_of, (TILE, WIDE)], 8,
    )
    sums = sum_of(sums, across(sums))
    bit = depth // 2
    while bit:
        sums = sum_of(sums, swap(sums, 4 * bit))
        bit //= 2
    sums = sum_of(sums, swap(sums, 2))
    sums = (sums, swap(sums, 1))

    held = {0: grad}
    bit = depth // 2
    while bit:
        for k in sorted(held):
            held[k ^ bit] = swap(held[k], 4 * bit)
        bit //= 2
    blocks, places = [], []
    for k in range(depth):
        for j, value in enumerate((held[k], swap(held[k], 2))):
            blocks += [value, swap(value, 1)]
            places += [(k, j, 0), (k, j, 1)]
    entries = full * rank
    out, late = early_update(places[:-2], places[-2:], sums, factor, blocks[:-2], entries)
    return late_update(places[-2:], sums, late, blocks[-2:], out, entries)


def solution(mesh):
    placed = (P("samples", "feat"), P("feat", None))
    return jax.shard_map(
        gradient_step, mesh=mesh, in_specs=placed, out_specs=P("feat", None), check_vma=False
    )
```
